128 devices in a mesh: shard: 8 (over y, core), tensor: 4 (over x), section: 4 (over z).
Axes of the slice: x: 4, y: 4, z: 4, core: 2. Of those that a mesh axis runs over, the one named last changes fastest.
Arguments:
- grad_square: bfloat16 [12, 4, 768, 768], P(None, None, ('shard', 'section'), 'tensor'), may hold values from -300 to 300
- grad_wide: bfloat16 [12, 2, 768, 3072], P(None, None, ('shard', 'section'), 'tensor'), may hold values from -300 to 300
- momentum_square: float32 [12, 4, 768, 768], P(None, None, ('shard', 'section'), 'tensor'), may hold values from -6 to 6
- momentum_wide: float32 [12, 2, 768, 3072], P(None, None, ('shard', 'section'), 'tensor'), may hold values from -6 to 6
- weights_square: float32 [12, 4, 768, 768], P(None, None, ('shard', 'section'), 'tensor'), may hold values from -0.21875 to 0.21875
- weights_wide: float32 [12, 2, 768, 3072], P(None, None, ('shard', 'section'), 'tensor'), may hold values from -0.21875 to 0.21875
Outputs:
- new_momentum_square: float32 [12, 4, 768, 768], P(None, None, ('shard', 'section'), 'tensor')
- new_momentum_wide: float32 [12, 2, 768, 3072], P(None, None, ('shard', 'section'), 'tensor')
- update_square: bfloat16 [12, 4, 768, 768], P(None, None, ('shard', 'section'), 'tensor')
- update_wide: bfloat16 [12, 2, 768, 3072], P(None, None, ('shard', 'section'), 'tensor')
- new_weights_square: float32 [12, 4, 768, 768], P(None, None, ('shard', 'section'), 'tensor')
- new_weights_wide: float32 [12, 2, 768, 3072], P(None, None, ('shard', 'section'), 'tensor')
The draws below stay inside these ranges and needn't reach their ends.
All inputs are finite; a program needn't handle non-finite values.
Results may differ from the reference program's by a relative error of at most 0.014.
Values may be sent and summed in bfloat16 or wider, within the bound.
A program may use at most 128 MiB of HBM per device.

```python
import math
import jax
import jax.numpy as jnp
from jax import lax

D = 768
FF = 3072
LAYERS = 12
ITERS = 3


def scaled_draw(key, shape):
    keys = jax.random.split(key, 3)
    low_row, high_row = (0.3, 3.0)
    rising = 10.0
    noise = jnp.clip(jax.random.normal(keys[0], shape, jnp.float32), -5.0, 5.0)
    row_scale = jnp.exp(jax.random.uniform(keys[1], shape[:-1] + (1,), jnp.float32, math.log(low_row), math.log(high_row)))
    col_scale = jnp.exp(jax.random.uniform(keys[2], shape[:-2] + (1, shape[-1]), jnp.float32, math.log(0.3), math.log(3.0)))
    position = jnp.arange(shape[-1], dtype=jnp.float32) / float(shape[-1] - 1) - 0.5
    ramp = jnp.exp(math.log(rising) * position)
    return noise * row_scale * col_scale * ramp


def draw_grad_square(key, part):
    return scaled_draw(jax.random.fold_in(key, 11), (LAYERS, 4, D, D)).astype(jnp.bfloat16)


def draw_grad_wide(key, part):
    return scaled_draw(jax.random.fold_in(key, 23), (LAYERS, 2, D, FF)).astype(jnp.bfloat16)


def steps_of(rng, dims, cuts, least, largest):
    def one(axis_at, shards_of):
        steps = jax.random.uniform(jax.random.fold_in(jax.random.fold_in(rng, 6), axis_at), (shards_of,), jnp.float32, least / len(cuts), largest / len(cuts))
        return jnp.repeat(jnp.exp(steps), dims[axis_at] // shards_of).reshape((-1,) + (1,) * (len(dims) - axis_at - 1))

    factor_of = one(*cuts[0])
    for cut in cuts[1:]:
        factor_of = factor_of * one(*cut)
    return factor_of


def scatter_about(own_key, extent, deviation, reach, shards=(), kind=jnp.bfloat16):
    result = deviation * jax.random.normal(own_key, extent, jnp.float32)
    if shards:
        result = result * steps_of(own_key, extent, shards, -0.22, 0.18)
    return jnp.clip(result, -reach, reach).astype(kind)


def setup_inputs(seed: int = 0) -> dict:
    streams_of = jax.random.split(jax.random.key(seed), 7)
    return {
        "grad_square": draw_grad_square(jax.random.fold_in(streams_of[6], 71), 0),
        "grad_wide": draw_grad_wide(jax.random.fold_in(streams_of[6], 71), 0),
        "momentum_square": scatter_about(streams_of[2], (LAYERS, 4, D, D), 1.0, 6.0, ((2, 32), (3, 4)), jnp.float32),
        "momentum_wide": scatter_about(streams_of[3], (LAYERS, 2, D, FF), 1.0, 6.0, ((2, 32), (3, 4)), jnp.float32),
        "weights_square": scatter_about(streams_of[4], (LAYERS, 4, D, D), D ** -0.5, 0.21875, ((2, 32), (3, 4)), jnp.float32),
        "weights_wide": scatter_about(streams_of[5], (LAYERS, 2, D, FF), D ** -0.5, 0.21875, ((2, 32), (3, 4)), jnp.float32),
    }


momentum_beta = 0.95
norm_epsilon = 1e-07
learning_rate = 0.02
weight_decay = 0.01
quintic_first = 3.4445
quintic_second = -4.775
quintic_third = 2.0315

def orthogonalize(start):
    widened = start.astype(jnp.float32)
    total = jnp.sum(widened * widened)
    matrix = (widened / (jnp.sqrt(total) + norm_epsilon)).astype(jnp.bfloat16)
    for sweep in range(ITERS):
        gram = lax.dot_general(matrix, matrix, (((1,), (1,)), ((), ())), preferred_element_type=jnp.float32).astype(jnp.bfloat16)
        squared = jnp.dot(gram, gram, preferred_element_type=jnp.float32)
        mixer = (quintic_second * gram.astype(jnp.float32) + quintic_third * squared).astype(jnp.bfloat16)
        matrix = (quintic_first * matrix.astype(jnp.float32) + jnp.dot(mixer, matrix, preferred_element_type=jnp.float32)).astype(jnp.bfloat16)
    factor = 0.2 * math.sqrt(max(start.shape))
    return (factor * matrix.astype(jnp.float32)).astype(jnp.bfloat16)

def one_kind(gradient, momentum, weights):
    moment_new = momentum_beta * momentum + gradient.astype(jnp.float32)
    start = (gradient.astype(jnp.float32) + momentum_beta * moment_new).astype(jnp.bfloat16)
    stacked = start.reshape((start.shape[0] * start.shape[1],) + start.shape[2:])
    updates = lax.map(orthogonalize, stacked).reshape(start.shape)
    weights_new = weights * (1.0 - learning_rate * weight_decay) - learning_rate * updates.astype(jnp.float32)
    return (moment_new, updates, weights_new)

def reference(grad_square, grad_wide, momentum_square, momentum_wide, weights_square, weights_wide):
    moment_sq, update_sq, weight_sq = one_kind(grad_square, momentum_square, weights_square)
    moment_wd, update_wd, weight_wd = one_kind(grad_wide, momentum_wide, weights_wide)
    return (moment_sq, moment_wd, update_sq, update_wd, weight_sq, weight_wd)
```

```python
import math

import jax
import jax.numpy as jnp
from jax import lax
from jax.experimental import pallas as pl
from jax.experimental.pallas import tpu as pltpu
from jax.sharding import PartitionSpec as P

momentum_beta = 0.95
norm_epsilon = 1e-07
learning_rate = 0.02
weight_decay = 0.01
qa = 3.4445
qb = -4.775
qc = 2.0315

MESH = pl.DeviceIdType.MESH
HALF = 384


def kernel(
    st_sq, st_wd, up_sq, up_wd,
    got_sq, got_wd, out_sq, out_wd, g32, part_out, part_in, b0, b1, b2, b3, b4,
    send1, recv1, own1, send2, recv2, own2, send_p, recv_p,
):
    sh, te, se = lax.axis_index("shard"), lax.axis_index("tensor"), lax.axis_index("section")
    core, yy = lax.rem(sh, 2), sh // 2
    row = sh * 4 + se
    f32, bf16 = jnp.float32, jnp.bfloat16

    barrier = pltpu.get_barrier_semaphore()
    for i in range(1, 128):
        a, b, c = i // 16, (i // 4) % 4, i % 4
        pl.semaphore_signal(
            barrier, inc=1,
            device_id=(lax.rem(sh + a, 8), lax.rem(te + b, 4), lax.rem(se + c, 4)),
            device_id_type=MESH,
        )
    pl.semaphore_wait(barrier, 127)

    u = lax.rem(se - te - yy + 8, 4)
    odd = lax.rem(te + yy, 2)
    is_wide = jnp.logical_or(u == 0, jnp.logical_and(u == 2, odd == 0))
    is_sq = jnp.logical_or(
        jnp.logical_and(lax.rem(u, 2) == 1, core == 0), jnp.logical_and(u == 2, odd == 1)
    )
    own_w = jnp.logical_and(is_wide, te // 2 == core)

    def put(src, dst, k, send, recv, own, dsh, dte, dse):
        mine = jnp.logical_and(jnp.logical_and(dsh == sh, dte == te), dse == se)

        @pl.when(mine)
        def _():
            pltpu.make_async_copy(src, dst, own.at[k]).start()

        @pl.when(jnp.logical_not(mine))
        def _():
            pltpu.make_async_remote_copy(
                src_ref=src, dst_ref=dst, send_sem=send.at[k], recv_sem=recv.at[k],
                device_id=(dsh, dte, dse), device_id_type=MESH,
            ).start()

    def all_of(ref, send, recv, k):
        return pltpu.make_async_remote_copy(
            src_ref=ref, dst_ref=ref, send_sem=send.at[k], recv_sem=recv.at[k],
            device_id=(sh, te, se), device_id_type=MESH,
        )

    def line(e):
        return lax.rem(te + lax.rem(e, 4), 4), lax.rem(yy + e // 4, 4)

    def line_of(l, parity):
        y = lax.rem(yy + l // 2, 4)
        return lax.rem(2 * lax.rem(l, 2) + te + lax.rem(te + y + parity, 2), 4), y

    def wide_to(xy, late):
        x, y = xy
        w = 16 + 2 * y + x // 2 if late else x + 4 * y
        put(
            st_wd.at[w], got_wd.at[lax.rem(te, 2) * 32 + row], 1, send1, recv1, own1,
            y * 2 + te // 2, x, lax.rem(x + y + 2 * late, 4),
        )

    def square_to(xy, g, c):
        x, y = xy
        s = 32 + (2 * y + x // 2) * 2 + c if g == 2 else x + 4 * y + 16 * g
        put(
            st_sq.at[s], got_sq.at[te * 32 + row], 0, send1, recv1, own1,
            y * 2 + c, x, lax.rem(x + y + (1, 3, 2)[g], 4),
        )

    def send_round(i, carry):
        q = lax.rem(i + 2 * se + 4 * core, 8)
        for j in range(2):
            square_to(line(2 * q + j), 0, 0)
            square_to(line(lax.rem(2 * q + j + 8, 16)), 1, 0)
            square_to(line_of(q, 1), 2, lax.rem(j + core, 2))
        wide_to(line(2 * q), 0)
        wide_to(line(2 * q + 1), 0)
        wide_to(line_of(lax.rem(q + 3, 8), 0), 1)
        return carry

    lax.fori_loop(0, 8, send_round, 0)

    def halves(body, init=0):
        def one(i, carry):
            return body(i, pl.ds(pl.multiple_of(i * HALF, HALF), HALF), carry)

        return lax.fori_loop(0, 2, one, init)

    def diag_sum(i, block):
        r = lax.broadcasted_iota(jnp.int32, block.shape, 0) + i * HALF
        c = lax.broadcasted_iota(jnp.int32, block.shape, 1)
        return jnp.sum(jnp.where(r == c, block, 0.0), keepdims=True)

    def flip(a, b):
        return lax.dot_general(a, b, (((1,), (1,)), ((), ())), preferred_element_type=f32)

    def rows_of(ref, j, i):
        return ref[pl.ds(j * 32 + i * 16, 16)].reshape(HALF, ref.shape[2])

    def block_of(ref, j):
        return ref[pl.ds(j * 32, 32)].reshape(768, ref.shape[2])

    @pl.when(is_sq)
    def _():
        pltpu.make_async_copy(st_sq.at[0], got_sq.at[0], own1.at[0]).wait()
        all_of(got_sq.at[pl.ds(0, 127)], send1, recv1, 0).wait_recv()

        def gram(i, rows, carry):
            total = flip(rows_of(got_sq, 0, i), block_of(got_sq, 0))
            for x in range(1, 4):
                total += flip(rows_of(got_sq, x, i), block_of(got_sq, x))
            g32[rows, :] = total
            part_in[rows, :] = jnp.zeros((HALF, 768), bf16)
            return carry

        halves(gram)

    @pl.when(is_wide)
    def _():
        @pl.when(own_w)
        def _():
            pltpu.make_async_copy(st_wd.at[0], got_wd.at[0], own1.at[1]).wait()
            all_of(got_wd.at[pl.ds(0, 63)], send1, recv1, 1).wait_recv()

        @pl.when(jnp.logical_not(own_w))
        def _():
            all_of(got_wd, send1, recv1, 1).wait_recv()

        def swap(i, rows):
            return pltpu.make_async_remote_copy(
                src_ref=part_out.at[rows, :], dst_ref=part_in.at[rows, :],
                send_sem=send_p.at[i], recv_sem=recv_p.at[i],
                device_id=(sh + 1 - 2 * core, te, se), device_id_type=MESH,
            )

        def gram(i, rows, carry):
            total = flip(rows_of(got_wd, 0, i), block_of(got_wd, 0))
            total += flip(rows_of(got_wd, 1, i), block_of(got_wd, 1))
            g32[rows, :] = total
            part_out[rows, :] = total.astype(bf16)
            swap(i, rows).start()
            return carry

        halves(gram)

        def swapped(i, rows, carry):
            swap(i, rows).wait()
            return carry

        halves(swapped)

    def step(dst, left, right, gain, *terms):
        def one(i, rows, carry):
            y = gain * jnp.dot(left[rows, :], right[...], preferred_element_type=f32)
            for weight, term in terms:
                y += weight * term[rows, :].astype(f32)
            dst[rows, :] = y.astype(bf16)
            return carry

        halves(one)

    @pl.when(jnp.logical_or(is_sq, is_wide))
    def _():
        def trace(i, rows, carry):
            block = g32[rows, :] + part_in[rows, :].astype(f32)
            g32[rows, :] = block
            return carry + diag_sum(i, block)

        total = halves(trace, jnp.zeros((1, 1), f32))
        scale = 1.0 / (jnp.sqrt(total) + norm_epsilon)

        def normalize(i, rows, carry):
            b0[rows, :] = (g32[rows, :] * scale * scale).astype(bf16)
            return carry

        halves(normalize)
        step(b1, b0, b0, qc, (qb, b0))
        step(b2, b1, b0, 1.0, (qa, b0))
        step(b3, b1, b2, 1.0, (qa, b2))
        step(b4, b3, b3, qc, (qb, b3))
        step(b0, b4, b1, 1.0, (qa, b1), (qa, b4))
        step(b2, b4, b3, 1.0, (qa, b3))
        step(b1, b4, b2, 1.0, (qa, b2))
        step(b3, b1, b1, qc, (qb, b1))
        step(b4, b3, b0, 1.0, (qa, b0), (qa * qa, b3))

        def apply(got, out, block, i, rows, factor):
            x = rows_of(got, block, i).astype(f32)
            y = jnp.dot(b4[rows, :], block_of(got, block), preferred_element_type=f32) + qa**3 * x
            y = (y * (scale * factor)).reshape(16, 24, got.shape[2])
            out[pl.ds(block * 32 + i * 16, 16)] = y.astype(bf16)

        @pl.when(is_sq)
        def _():
            s = jnp.where(
                u == 2, 32 + (2 * yy + te // 2) * 2 + core, te + 4 * yy + 16 * (u // 2)
            )

            def back(k, carry):
                x, i = lax.rem(k // 2 + te, 4), lax.rem(k, 2)
                apply(got_sq, out_sq, x, i, pl.ds(pl.multiple_of(i * HALF, HALF), HALF), 0.2 * math.sqrt(768))

                def piece(t, c2):
                    r = i * 16 + lax.rem(t + 4 * yy + se, 16)
                    put(
                        out_sq.at[x * 32 + r], up_sq.at[s], 0, send2, recv2, own2,
                        r // 4, x, lax.rem(r, 4),
                    )
                    return c2

                lax.fori_loop(0, 16, piece, 0)
                return carry

            lax.fori_loop(0, 8, back, 0)

        @pl.when(is_wide)
        def _():
            w = jnp.where(u == 2, 16 + 2 * yy + te // 2, te + 4 * yy)

            def back(k, carry):
                x, i = lax.rem(k // 2 + te, 2), lax.rem(k, 2)
                apply(got_wd, out_wd, x, i, pl.ds(pl.multiple_of(i * HALF, HALF), HALF), 0.2 * math.sqrt(3072))

                def piece(t, c2):
                    r = i * 16 + lax.rem(t + 4 * yy + se, 16)
                    put(
                        out_wd.at[x * 32 + r], up_wd.at[w], 1, send2, recv2, own2,
                        r // 4, 2 * core + x, lax.rem(r, 4),
                    )
                    return c2

                lax.fori_loop(0, 16, piece, 0)
                return carry

            lax.fori_loop(0, 4, back, 0)

    @pl.when(is_sq)
    def _():
        pltpu.make_async_copy(out_sq.at[0], up_sq.at[0], own2.at[0]).wait()
        all_of(st_sq.at[pl.ds(0, 47)], send1, recv1, 0).wait_send()
        all_of(out_sq.at[pl.ds(0, 127)], send2, recv2, 0).wait_send()
        all_of(up_sq.at[pl.ds(0, 47)], send2, recv2, 0).wait_recv()

    @pl.when(jnp.logical_not(is_sq))
    def _():
        all_of(st_sq, send1, recv1, 0).wait_send()
        all_of(up_sq, send2, recv2, 0).wait_recv()

    @pl.when(own_w)
    def _():
        pltpu.make_async_copy(out_wd.at[0], up_wd.at[0], own2.at[1]).wait()
        all_of(st_wd.at[pl.ds(0, 23)], send1, recv1, 1).wait_send()
        all_of(out_wd.at[pl.ds(0, 63)], send2, recv2, 1).wait_send()
        all_of(up_wd.at[pl.ds(0, 23)], send2, recv2, 1).wait_recv()

    @pl.when(jnp.logical_not(own_w))
    def _():
        all_of(st_wd, send1, recv1, 1).wait_send()
        all_of(up_wd, send2, recv2, 1).wait_recv()

    @pl.when(jnp.logical_and(is_wide, jnp.logical_not(own_w)))
    def _():
        all_of(out_wd, send2, recv2, 1).wait_send()


def orthogonalize(start_sq, start_wd):
    any_space = pl.BlockSpec(memory_space=pl.ANY)
    vmem = pltpu.VMEM
    bf16 = jnp.bfloat16
    pair = pltpu.SemaphoreType.DMA((2,))
    return pl.pallas_call(
        kernel,
        out_shape=(
            jax.ShapeDtypeStruct((48, 24, 192), bf16),
            jax.ShapeDtypeStruct((24, 24, 768), bf16),
        ),
        in_specs=[any_space] * 2,
        out_specs=[any_space] * 2,
        scratch_shapes=[
            vmem((128, 24, 192), bf16), vmem((64, 24, 768), bf16),
            vmem((128, 24, 192), bf16), vmem((64, 24, 768), bf16),
            vmem((768, 768), jnp.float32), vmem((768, 768), bf16), vmem((768, 768), bf16),
        ] + [vmem((768, 768), bf16)] * 5 + [pair] * 8,
        compiler_params=pltpu.CompilerParams(collective_id=0, has_side_effects=True),
    )(start_sq, start_wd)


def local(grad_square, grad_wide, momentum_square, momentum_wide, weights_square, weights_wide):
    moment_sq = momentum_beta * momentum_square + grad_square.astype(jnp.float32)
    moment_wd = momentum_beta * momentum_wide + grad_wide.astype(jnp.float32)
    start_sq = (grad_square.astype(jnp.float32) + momentum_beta * moment_sq).astype(jnp.bfloat16)
    start_wd = (grad_wide.astype(jnp.float32) + momentum_beta * moment_wd).astype(jnp.bfloat16)
    update_sq, update_wd = orthogonalize(
        start_sq.reshape(48, 24, 192), start_wd.reshape(24, 24, 768)
    )
    update_sq = update_sq.reshape(start_sq.shape)
    update_wd = update_wd.reshape(start_wd.shape)
    keep = 1.0 - learning_rate * weight_decay
    weight_sq = weights_square * keep - learning_rate * update_sq.astype(jnp.float32)
    weight_wd = weights_wide * keep - learning_rate * update_wd.astype(jnp.float32)
    return (moment_sq, moment_wd, update_sq, update_wd, weight_sq, weight_wd)


def solution(mesh):
    spec = P(None, None, ("shard", "section"), "tensor")
    return jax.shard_map(
        local, mesh=mesh, in_specs=(spec,) * 6, out_specs=(spec,) * 6, check_vma=False
    )
```

```python
import math

import jax
import jax.numpy as jnp
from jax import lax
from jax.experimental import pallas as pl
from jax.experimental.pallas import tpu as pltpu
from jax.sharding import PartitionSpec as P

momentum_beta = 0.95
norm_epsilon = 1e-07
learning_rate = 0.02
weight_decay = 0.01
qa = 3.4445
qb = -4.775
qc = 2.0315

MESH = pl.DeviceIdType.MESH
HALF = 384


def kernel(
    st_sq, st_wd, up_sq, up_wd,
    got_sq, got_wd, out_sq, out_wd, via1, via2, trace, g32, part_out, part_in, b0, b1, b2, b3, b4,
    send1, recv1, own1, send2, recv2, own2, send_p, recv_p, sent_v, recv_v1, recv_v2,
):
    sh, te, se = lax.axis_index("shard"), lax.axis_index("tensor"), lax.axis_index("section")
    core, yy = lax.rem(sh, 2), sh // 2
    row = sh * 4 + se
    f32, bf16 = jnp.float32, jnp.bfloat16

    barrier = pltpu.get_barrier_semaphore()
    for i in range(1, 128):
        a, b, c = i // 16, (i // 4) % 4, i % 4
        pl.semaphore_signal(
            barrier, inc=1,
            device_id=(lax.rem(sh + a, 8), lax.rem(te + b, 4), lax.rem(se + c, 4)),
            device_id_type=MESH,
        )
    pl.semaphore_wait(barrier, 127)

    u = lax.rem(se - te - yy + 8, 4)
    odd = lax.rem(te + yy, 2)
    is_wide = jnp.logical_or(u == 0, jnp.logical_and(u == 2, odd == 0))
    is_sq = jnp.logical_or(
        jnp.logical_and(lax.rem(u, 2) == 1, core == 0), jnp.logical_and(u == 2, odd == 1)
    )
    own_w = jnp.logical_and(is_wide, te // 2 == core)
    near_z = se + 1 - 2 * lax.rem(se, 2)

    def wide_at(x, y, z):
        v = lax.rem(z - x - y + 8, 4)
        return jnp.logical_or(v == 0, jnp.logical_and(v == 2, lax.rem(x + y, 2) == 0))

    def wide_of(x, y, z):
        v = lax.rem(z - x - y + 8, 4)
        return (1 - v // 2) * (x + 4 * y) + (v // 2) * (16 + 2 * y + x // 2)

    spare = jnp.logical_and(lax.rem(u, 2) == 1, core == 1)
    via_in = jnp.logical_and(spare, wide_at(te, yy, near_z))
    via_out = jnp.logical_and(spare, wide_at(3 - te, yy, se))

    def put(src, dst, k, send, recv, own, dsh, dte, dse):
        mine = jnp.logical_and(jnp.logical_and(dsh == sh, dte == te), dse == se)

        @pl.when(mine)
        def _():
            pltpu.make_async_copy(src, dst, own.at[k]).start()

        @pl.when(jnp.logical_not(mine))
        def _():
            pltpu.make_async_remote_copy(
                src_ref=src, dst_ref=dst, send_sem=send.at[k], recv_sem=recv.at[k],
                device_id=(dsh, dte, dse), device_id_type=MESH,
            ).start()

    def all_of(ref, send, recv, k):
        return pltpu.make_async_remote_copy(
            src_ref=ref, dst_ref=ref, send_sem=send.at[k], recv_sem=recv.at[k],
            device_id=(sh, te, se), device_id_type=MESH,
        )

    def line(e):
        return lax.rem(te + lax.rem(e, 4), 4), lax.rem(yy + e // 4, 4)

    def line_of(l, parity):
        y = lax.rem(yy + l // 2, 4)
        return lax.rem(2 * lax.rem(l, 2) + te + lax.rem(te + y + parity, 2), 4), y

    def wide_to(xy, late):
        x, y = xy
        w = 16 + 2 * y + x // 2 if late else x + 4 * y
        z = lax.rem(x + y + 2 * late, 4)
        around = jnp.logical_and(core == 1, lax.rem(z + 2, 4) == se)

        @pl.when(around)
        def _():
            slot = te * 4 + yy
            pltpu.make_async_remote_copy(
                src_ref=st_wd.at[w], dst_ref=via1.at[slot],
                send_sem=send1.at[1], recv_sem=recv_v1.at[slot],
                device_id=(2 * y + 1, x, z + 1 - 2 * lax.rem(z, 2)), device_id_type=MESH,
            ).start()

        @pl.when(jnp.logical_not(around))
        def _():
            put(
                st_wd.at[w], got_wd.at[lax.rem(te, 2) * 32 + row], 1, send1, recv1, own1,
                y * 2 + te // 2, x, z,
            )

    def square_to(xy, g, c):
        x, y = xy
        s = 32 + (2 * y + x // 2) * 2 + c if g == 2 else x + 4 * y + 16 * g
        put(
            st_sq.at[s], got_sq.at[te * 32 + row], 0, send1, recv1, own1,
            y * 2 + c, x, lax.rem(x + y + (1, 3, 2)[g], 4),
        )

    def send_wides(i, carry):
        q = lax.rem(i + 2 * se + 4 * core, 8)
        wide_to(line(2 * q), 0)
        wide_to(line(2 * q + 1), 0)
        wide_to(line_of(lax.rem(q + 3, 8), 0), 1)
        return carry

    def send_squares(i, carry):
        q = lax.rem(i + 2 * se + 4 * core, 8)
        for j in range(2):
            square_to(line(2 * q + j), 0, 0)
            square_to(line(lax.rem(2 * q + j + 8, 16)), 1, 0)
            square_to(line_of(q, 1), 2, lax.rem(j + core, 2))
        return carry

    lax.fori_loop(0, 8, send_wides, 0)
    lax.fori_loop(0, 8, send_squares, 0)

    @pl.when(via_in)
    def _():
        def onward(slot, carry):
            x = slot // 4
            far_row = (2 * lax.rem(slot, 4) + 1) * 4 + lax.rem(near_z + 2, 4)
            copy = pltpu.make_async_remote_copy(
                src_ref=via1.at[slot], dst_ref=via1.at[slot],
                send_sem=sent_v.at[0], recv_sem=recv_v1.at[slot],
                device_id=(sh, te, se), device_id_type=MESH,
            )
            copy.wait_recv()
            pltpu.make_async_remote_copy(
                src_ref=via1.at[slot], dst_ref=got_wd.at[lax.rem(x, 2) * 32 + far_row],
                send_sem=sent_v.at[0], recv_sem=recv1.at[1],
                device_id=(2 * yy + x // 2, te, near_z), device_id_type=MESH,
            ).start()
            return carry

        lax.fori_loop(0, 16, onward, 0)

    @pl.when(via_out)
    def _():
        w_far = wide_of(3 - te, yy, se)

        def onward(slot, carry):
            copy = pltpu.make_async_remote_copy(
                src_ref=via2.at[slot], dst_ref=via2.at[slot],
                send_sem=sent_v.at[1], recv_sem=recv_v2.at[slot],
                device_id=(sh, te, se), device_id_type=MESH,
            )
            copy.wait_recv()
            pltpu.make_async_remote_copy(
                src_ref=via2.at[slot], dst_ref=up_wd.at[w_far],
                send_sem=sent_v.at[1], recv_sem=recv2.at[1],
                device_id=(2 * (slot // 4) + 1, lax.rem(5 - te, 4), lax.rem(slot, 4)),
                device_id_type=MESH,
            ).start()
            return carry

        lax.fori_loop(0, 16, onward, 0)

    def halves(body, init=0):
        def one(i, carry):
            return body(i, pl.ds(pl.multiple_of(i * HALF, HALF), HALF), carry)

        return lax.fori_loop(0, 2, one, init)

    def diag_sum(i, block):
        r = lax.broadcasted_iota(jnp.int32, block.shape, 0) + i * HALF
        c = lax.broadcasted_iota(jnp.int32, block.shape, 1)
        return jnp.sum(jnp.where(r == c, block, 0.0), keepdims=True)

    def flip(a, b):
        return lax.dot_general(a, b, (((1,), (1,)), ((), ())), preferred_element_type=f32)

    def rows_of(ref, j, i):
        return ref[pl.ds(j * 32 + i * 16, 16)].reshape(HALF, ref.shape[2])

    def block_of(ref, j):
        return ref[pl.ds(j * 32, 32)].reshape(768, ref.shape[2])

    @pl.when(is_sq)
    def _():
        pltpu.make_async_copy(st_sq.at[0], got_sq.at[0], own1.at[0]).wait()
        all_of(got_sq.at[pl.ds(0, 127)], send1, recv1, 0).wait_recv()

        def gram(i, rows, carry):
            total = flip(rows_of(got_sq, 0, i), block_of(got_sq, 0))
            for x in range(1, 4):
                total += flip(rows_of(got_sq, x, i), block_of(got_sq, x))
            b0[rows, :] = total.astype(bf16)
            return carry + diag_sum(i, total)

        trace[...] = jnp.broadcast_to(halves(gram, jnp.zeros((1, 1), f32)), trace.shape)

    @pl.when(is_wide)
    def _():
        @pl.when(own_w)
        def _():
            pltpu.make_async_copy(st_wd.at[0], got_wd.at[0], own1.at[1]).wait()
            all_of(got_wd.at[pl.ds(0, 63)], send1, recv1, 1).wait_recv()

        @pl.when(jnp.logical_not(own_w))
        def _():
            all_of(got_wd, send1, recv1, 1).wait_recv()

        def swap(i, rows):
            return pltpu.make_async_remote_copy(
                src_ref=part_out.at[rows, :], dst_ref=part_in.at[rows, :],
                send_sem=send_p.at[i], recv_sem=recv_p.at[i],
                device_id=(sh + 1 - 2 * core, te, se), device_id_type=MESH,
            )

        def gram(i, rows, carry):
            total = flip(rows_of(got_wd, 0, i), block_of(got_wd, 0))
            total += flip(rows_of(got_wd, 1, i), block_of(got_wd, 1))
            g32[rows, :] = total
            part_out[rows, :] = total.astype(bf16)
            swap(i, rows).start()
            return carry

        halves(gram)

        def swapped(i, rows, carry):
            swap(i, rows).wait()
            total = g32[rows, :] + part_in[rows, :].astype(f32)
            b0[rows, :] = total.astype(bf16)
            return carry + diag_sum(i, total)

        trace[...] = jnp.broadcast_to(halves(swapped, jnp.zeros((1, 1), f32)), trace.shape)

    def step(dst, left, right, gain, *terms):
        def one(i, rows, carry):
            y = gain * jnp.dot(left[rows, :], right[...], preferred_element_type=f32)
            for weight, term in terms:
                y += weight * term[rows, :].astype(f32)
            dst[rows, :] = y.astype(bf16)
            return carry

        halves(one)

    @pl.when(jnp.logical_or(is_sq, is_wide))
    def _():
        scale = 1.0 / (jnp.sqrt(trace[0:1, 0:1]) + norm_epsilon)
        gain = scale * scale
        step(b1, b0, b0, qc * gain * gain, (qb * gain, b0))
        step(b2, b1, b0, gain, (qa * gain, b0))
        step(b3, b1, b2, 1.0, (qa, b2))
        step(b4, b3, b3, qc, (qb, b3))
        step(b0, b4, b1, 1.0, (qa, b1), (qa, b4))
        step(b2, b4, b3, 1.0, (qa, b3))
        step(b1, b4, b2, 1.0, (qa, b2))
        step(b3, b1, b1, qc, (qb, b1))
        step(b4, b3, b0, 1.0, (qa, b0), (qa * qa, b3))

        def apply(got, out, block, i, rows):
            x = rows_of(got, block, i).astype(f32)
            y = jnp.dot(b4[rows, :], block_of(got, block), preferred_element_type=f32) + qa**3 * x
            y = (y * scale).reshape(16, 24, got.shape[2])
            out[pl.ds(block * 32 + i * 16, 16)] = y.astype(bf16)

        @pl.when(is_sq)
        def _():
            s = jnp.where(
                u == 2, 32 + (2 * yy + te // 2) * 2 + core, te + 4 * yy + 16 * (u // 2)
            )

            def back(k, carry):
                x, i = lax.rem(k // 2 + te, 4), lax.rem(k, 2)
                apply(got_sq, out_sq, x, i, pl.ds(pl.multiple_of(i * HALF, HALF), HALF))

                def piece(t, c2):
                    r = i * 16 + lax.rem(t + 4 * yy + se, 16)
                    put(
                        out_sq.at[x * 32 + r], up_sq.at[s], 0, send2, recv2, own2,
                        r // 4, x, lax.rem(r, 4),
                    )
                    return c2

                lax.fori_loop(0, 16, piece, 0)
                return carry

            lax.fori_loop(0, 8, back, 0)

        @pl.when(is_wide)
        def _():
            w = wide_of(te, yy, se)

            def back(k, carry):
                x, i = lax.rem(k // 2 + te, 2), lax.rem(k, 2)
                apply(got_wd, out_wd, x, i, pl.ds(pl.multiple_of(i * HALF, HALF), HALF))

                def piece(t, c2):
                    r = i * 16 + lax.rem(t + 4 * yy + se, 16)
                    around = jnp.logical_and(
                        lax.rem(r // 4, 2) == 1, lax.rem(te + 2, 4) == 2 * core + x
                    )

                    @pl.when(around)
                    def _():
                        slot = r // 8 * 4 + lax.rem(r, 4)
                        pltpu.make_async_remote_copy(
                            src_ref=out_wd.at[x * 32 + r], dst_ref=via2.at[slot],
                            send_sem=send2.at[1], recv_sem=recv_v2.at[slot],
                            device_id=(2 * yy + 1, 3 - te, se), device_id_type=MESH,
                        ).start()

                    @pl.when(jnp.logical_not(around))
                    def _():
                        put(
                            out_wd.at[x * 32 + r], up_wd.at[w], 1, send2, recv2, own2,
                            r // 4, 2 * core + x, lax.rem(r, 4),
                        )

                    return c2

                lax.fori_loop(0, 16, piece, 0)
                return carry

            lax.fori_loop(0, 4, back, 0)

    @pl.when(is_sq)
    def _():
        pltpu.make_async_copy(out_sq.at[0], up_sq.at[0], own2.at[0]).wait()
        all_of(st_sq.at[pl.ds(0, 47)], send1, recv1, 0).wait_send()
        all_of(out_sq.at[pl.ds(0, 127)], send2, recv2, 0).wait_send()
        all_of(up_sq.at[pl.ds(0, 47)], send2, recv2, 0).wait_recv()

    @pl.when(jnp.logical_not(is_sq))
    def _():
        all_of(st_sq, send1, recv1, 0).wait_send()
        all_of(up_sq, send2, recv2, 0).wait_recv()

    @pl.when(own_w)
    def _():
        pltpu.make_async_copy(out_wd.at[0], up_wd.at[0], own2.at[1]).wait()
        all_of(st_wd.at[pl.ds(0, 23)], send1, recv1, 1).wait_send()
        all_of(out_wd.at[pl.ds(0, 63)], send2, recv2, 1).wait_send()
        all_of(up_wd.at[pl.ds(0, 23)], send2, recv2, 1).wait_recv()

    @pl.when(jnp.logical_not(own_w))
    def _():
        all_of(st_wd, send1, recv1, 1).wait_send()
        all_of(up_wd, send2, recv2, 1).wait_recv()

    @pl.when(jnp.logical_and(is_wide, jnp.logical_not(own_w)))
    def _():
        all_of(out_wd, send2, recv2, 1).wait_send()


    @pl.when(via_in)
    def _():
        all_of(via1, sent_v, recv1, 0).wait_send()

    @pl.when(via_out)
    def _():
        all_of(via2, sent_v, recv1, 1).wait_send()


def orthogonalize(start_sq, start_wd):
    any_space = pl.BlockSpec(memory_space=pl.ANY)
    vmem = pltpu.VMEM
    bf16 = jnp.bfloat16
    pair = pltpu.SemaphoreType.DMA((2,))
    return pl.pallas_call(
        kernel,
        out_shape=(
            jax.ShapeDtypeStruct((48, 24, 192), bf16),
            jax.ShapeDtypeStruct((24, 24, 768), bf16),
        ),
        in_specs=[any_space] * 2,
        out_specs=[any_space] * 2,
        scratch_shapes=[
            vmem((128, 24, 192), bf16), vmem((64, 24, 768), bf16),
            vmem((128, 24, 192), bf16), vmem((64, 24, 768), bf16),
            vmem((16, 24, 768), bf16), vmem((16, 24, 768), bf16), vmem((8, 128), jnp.float32),
            vmem((768, 768), jnp.float32), vmem((768, 768), bf16), vmem((768, 768), bf16),
        ] + [vmem((768, 768), bf16)] * 5 + [pair] * 9 + [pltpu.SemaphoreType.DMA((16,))] * 2,
        compiler_params=pltpu.CompilerParams(collective_id=0, has_side_effects=True),
    )(start_sq, start_wd)


def local(grad_square, grad_wide, momentum_square, momentum_wide, weights_square, weights_wide):
    moment_sq = momentum_beta * momentum_square + grad_square.astype(jnp.float32)
    moment_wd = momentum_beta * momentum_wide + grad_wide.astype(jnp.float32)
    start_sq = (grad_square.astype(jnp.float32) + momentum_beta * moment_sq).astype(jnp.bfloat16)
    start_wd = (grad_wide.astype(jnp.float32) + momentum_beta * moment_wd).astype(jnp.bfloat16)
    done_sq, done_wd = orthogonalize(
        start_sq.reshape(48, 24, 192), start_wd.reshape(24, 24, 768)
    )
    done_sq = done_sq.reshape(start_sq.shape).astype(jnp.float32)
    done_wd = done_wd.reshape(start_wd.shape).astype(jnp.float32)
    update_sq = (0.2 * math.sqrt(768) * done_sq).astype(jnp.bfloat16)
    update_wd = (0.2 * math.sqrt(3072) * done_wd).astype(jnp.bfloat16)
    keep = 1.0 - learning_rate * weight_decay
    weight_sq = weights_square * keep - learning_rate * update_sq.astype(jnp.float32)
    weight_wd = weights_wide * keep - learning_rate * update_wd.astype(jnp.float32)
    return (moment_sq, moment_wd, update_sq, update_wd, weight_sq, weight_wd)


def solution(mesh):
    spec = P(None, None, ("shard", "section"), "tensor")
    return jax.shard_map(
        local, mesh=mesh, in_specs=(spec,) * 6, out_specs=(spec,) * 6, check_vma=False
    )
```

```python
import math

import jax
import jax.numpy as jnp
from jax import lax
from jax.experimental import pallas as pl
from jax.experimental.pallas import tpu as pltpu
from jax.sharding import PartitionSpec as P

momentum_beta = 0.95
norm_epsilon = 1e-07
learning_rate = 0.02
weight_decay = 0.01
qa = 3.4445
qb = -4.775
qc = 2.0315

MESH = pl.DeviceIdType.MESH
HALF = 384


def kernel(
    st_sq, st_wd, up_sq, up_wd,
    got_sq, got_wd, out_sq, out_wd, via1, via2, trace, g32, part_out, part_in, b0, b1, b2, b3, b4,
    send1, recv1, own1, send2, recv2, own2, send_p, recv_p, sent_v, recv_v1, recv_v2,
):
    sh, te, se = lax.axis_index("shard"), lax.axis_index("tensor"), lax.axis_index("section")
    core, yy = lax.rem(sh, 2), sh // 2
    row = sh * 4 + se
    f32, bf16 = jnp.float32, jnp.bfloat16

    barrier = pltpu.get_barrier_semaphore()
    for i in range(1, 128):
        a, b, c = i // 16, (i // 4) % 4, i % 4
        pl.semaphore_signal(
            barrier, inc=1,
            device_id=(lax.rem(sh + a, 8), lax.rem(te + b, 4), lax.rem(se + c, 4)),
            device_id_type=MESH,
        )
    pl.semaphore_wait(barrier, 127)

    u = lax.rem(se - te - yy + 8, 4)
    odd = lax.rem(te + yy, 2)
    is_wide = jnp.logical_or(u == 0, jnp.logical_and(u == 2, odd == 0))
    is_sq = jnp.logical_or(
        jnp.logical_and(lax.rem(u, 2) == 1, core == 0), jnp.logical_and(u == 2, odd == 1)
    )
    own_w = jnp.logical_and(is_wide, te // 2 == core)
    near_z = se + 1 - 2 * lax.rem(se, 2)

    def wide_at(x, y, z):
        v = lax.rem(z - x - y + 8, 4)
        return jnp.logical_or(v == 0, jnp.logical_and(v == 2, lax.rem(x + y, 2) == 0))

    def wide_of(x, y, z):
        v = lax.rem(z - x - y + 8, 4)
        return (1 - v // 2) * (x + 4 * y) + (v // 2) * (16 + 2 * y + x // 2)

    spare = jnp.logical_and(lax.rem(u, 2) == 1, core == 1)
    via_in = jnp.logical_and(spare, wide_at(te, yy, near_z))
    via_out = jnp.logical_and(spare, wide_at(3 - te, yy, se))

    def put(src, dst, k, send, recv, own, dsh, dte, dse):
        mine = jnp.logical_and(jnp.logical_and(dsh == sh, dte == te), dse == se)

        @pl.when(mine)
        def _():
            pltpu.make_async_copy(src, dst, own.at[k]).start()

        @pl.when(jnp.logical_not(mine))
        def _():
            pltpu.make_async_remote_copy(
                src_ref=src, dst_ref=dst, send_sem=send.at[k], recv_sem=recv.at[k],
                device_id=(dsh, dte, dse), device_id_type=MESH,
            ).start()

    def all_of(ref, send, recv, k):
        return pltpu.make_async_remote_copy(
            src_ref=ref, dst_ref=ref, send_sem=send.at[k], recv_sem=recv.at[k],
            device_id=(sh, te, se), device_id_type=MESH,
        )

    def line(e):
        return lax.rem(te + lax.rem(e, 4), 4), lax.rem(yy + e // 4, 4)

    def line_of(l, parity):
        y = lax.rem(yy + l // 2, 4)
        return lax.rem(2 * lax.rem(l, 2) + te + lax.rem(te + y + parity, 2), 4), y

    def wide_to(xy, late):
        x, y = xy
        w = 16 + 2 * y + x // 2 if late else x + 4 * y
        z = lax.rem(x + y + 2 * late, 4)
        around = jnp.logical_and(jnp.logical_and(core == 1, yy < 3), lax.rem(z + 2, 4) == se)

        @pl.when(around)
        def _():
            slot = te * 3 + yy
            pltpu.make_async_remote_copy(
                src_ref=st_wd.at[w], dst_ref=via1.at[slot],
                send_sem=send1.at[1], recv_sem=recv_v1.at[slot],
                device_id=(2 * y + 1, x, z + 1 - 2 * lax.rem(z, 2)), device_id_type=MESH,
            ).start()

        @pl.when(jnp.logical_not(around))
        def _():
            put(
                st_wd.at[w], got_wd.at[lax.rem(te, 2) * 32 + row], 1, send1, recv1, own1,
                y * 2 + te // 2, x, z,
            )

    def square_to(xy, g, c):
        x, y = xy
        s = 32 + (2 * y + x // 2) * 2 + c if g == 2 else x + 4 * y + 16 * g
        put(
            st_sq.at[s], got_sq.at[te * 32 + row], 0, send1, recv1, own1,
            y * 2 + c, x, lax.rem(x + y + (1, 3, 2)[g], 4),
        )

    def send_wides(i, carry):
        q = lax.rem(i + 2 * se + 4 * core, 8)
        wide_to(line(2 * q), 0)
        wide_to(line(2 * q + 1), 0)
        wide_to(line_of(lax.rem(q + 3, 8), 0), 1)
        return carry

    def send_squares(i, carry):
        q = lax.rem(i + 2 * se + 4 * core, 8)
        for j in range(2):
            square_to(line(2 * q + j), 0, 0)
            square_to(line(lax.rem(2 * q + j + 8, 16)), 1, 0)
            square_to(line_of(q, 1), 2, lax.rem(j + core, 2))
        return carry

    lax.fori_loop(0, 8, send_wides, 0)

    @pl.when(via_in)
    def _():
        def onward(slot, carry):
            x = slot // 3
            far_row = (2 * lax.rem(slot, 3) + 1) * 4 + lax.rem(near_z + 2, 4)
            copy = pltpu.make_async_remote_copy(
                src_ref=via1.at[slot], dst_ref=via1.at[slot],
                send_sem=sent_v.at[0], recv_sem=recv_v1.at[slot],
                device_id=(sh, te, se), device_id_type=MESH,
            )
            copy.wait_recv()
            pltpu.make_async_remote_copy(
                src_ref=via1.at[slot], dst_ref=got_wd.at[lax.rem(x, 2) * 32 + far_row],
                send_sem=sent_v.at[0], recv_sem=recv1.at[1],
                device_id=(2 * yy + x // 2, te, near_z), device_id_type=MESH,
            ).start()
            return carry

        lax.fori_loop(0, 12, onward, 0)

    lax.fori_loop(0, 8, send_squares, 0)

    @pl.when(via_out)
    def _():
        w_far = wide_of(3 - te, yy, se)

        def onward(t, carry):
            r = t // 16 * 16 + lax.rem(t + 4 * yy + se, 16)

            @pl.when(lax.rem(r // 4, 2) == 1)
            def _():
                slot = r // 8 * 4 + lax.rem(r, 4)
                copy = pltpu.make_async_remote_copy(
                    src_ref=via2.at[slot], dst_ref=via2.at[slot],
                    send_sem=sent_v.at[1], recv_sem=recv_v2.at[slot],
                    device_id=(sh, te, se), device_id_type=MESH,
                )
                copy.wait_recv()
                pltpu.make_async_remote_copy(
                    src_ref=via2.at[slot], dst_ref=up_wd.at[w_far],
                    send_sem=sent_v.at[1], recv_sem=recv2.at[1],
                    device_id=(r // 4, lax.rem(5 - te, 4), lax.rem(r, 4)),
                    device_id_type=MESH,
                ).start()

            return carry

        lax.fori_loop(0, 32, onward, 0)

    def halves(body, init=0):
        def one(i, carry):
            return body(i, pl.ds(pl.multiple_of(i * HALF, HALF), HALF), carry)

        return lax.fori_loop(0, 2, one, init)

    def diag_sum(i, block):
        r = lax.broadcasted_iota(jnp.int32, block.shape, 0) + i * HALF
        c = lax.broadcasted_iota(jnp.int32, block.shape, 1)
        return jnp.sum(jnp.where(r == c, block, 0.0), keepdims=True)

    def flip(a, b):
        return lax.dot_general(a, b, (((1,), (1,)), ((), ())), preferred_element_type=f32)

    def rows_of(ref, j, i):
        return ref[pl.ds(j * 32 + i * 16, 16)].reshape(HALF, ref.shape[2])

    def block_of(ref, j):
        return ref[pl.ds(j * 32, 32)].reshape(768, ref.shape[2])

    @pl.when(is_sq)
    def _():
        pltpu.make_async_copy(st_sq.at[0], got_sq.at[0], own1.at[0]).wait()
        all_of(got_sq.at[pl.ds(0, 127)], send1, recv1, 0).wait_recv()

        def gram(i, rows, carry):
            total = flip(rows_of(got_sq, 0, i), block_of(got_sq, 0))
            for x in range(1, 4):
                total += flip(rows_of(got_sq, x, i), block_of(got_sq, x))
            b0[rows, :] = total.astype(bf16)
            return carry + diag_sum(i, total)

        trace[...] = jnp.broadcast_to(halves(gram, jnp.zeros((1, 1), f32)), trace.shape)

    @pl.when(is_wide)
    def _():
        @pl.when(own_w)
        def _():
            pltpu.make_async_copy(st_wd.at[0], got_wd.at[0], own1.at[1]).wait()
            all_of(got_wd.at[pl.ds(0, 63)], send1, recv1, 1).wait_recv()

        @pl.when(jnp.logical_not(own_w))
        def _():
            all_of(got_wd, send1, recv1, 1).wait_recv()

        def swap(i, rows):
            return pltpu.make_async_remote_copy(
                src_ref=part_out.at[rows, :], dst_ref=part_in.at[rows, :],
                send_sem=send_p.at[i], recv_sem=recv_p.at[i],
                device_id=(sh + 1 - 2 * core, te, se), device_id_type=MESH,
            )

        def gram(i, rows, carry):
            total = flip(rows_of(got_wd, 0, i), block_of(got_wd, 0))
            total += flip(rows_of(got_wd, 1, i), block_of(got_wd, 1))
            g32[rows, :] = total
            part_out[rows, :] = total.astype(bf16)
            swap(i, rows).start()
            return carry

        halves(gram)

        def swapped(i, rows, carry):
            swap(i, rows).wait()
            total = g32[rows, :] + part_in[rows, :].astype(f32)
            b0[rows, :] = total.astype(bf16)
            return carry + diag_sum(i, total)

        trace[...] = jnp.broadcast_to(halves(swapped, jnp.zeros((1, 1), f32)), trace.shape)

    def step(dst, left, right, gain, *terms):
        def part(rows, cols):
            y = gain * jnp.dot(left[rows, :], right[:, cols], preferred_element_type=f32)
            for weight, term in terms:
                y += weight * term[rows, cols].astype(f32)
            return y.astype(bf16)

        top, low = slice(0, HALF), slice(HALF, 768)
        upper = part(top, slice(0, 768))
        dst[top, :] = upper
        dst[low, top] = upper[:, HALF:].T
        dst[low, low] = part(low, low)

    @pl.when(jnp.logical_or(is_sq, is_wide))
    def _():
        scale = 1.0 / (jnp.sqrt(trace[0:1, 0:1]) + norm_epsilon)
        gain = scale * scale
        step(b1, b0, b0, qc * gain * gain, (qb * gain, b0))
        step(b2, b1, b0, gain, (qa * gain, b0))
        step(b3, b1, b2, 1.0, (qa, b2))
        step(b4, b3, b3, qc, (qb, b3))
        step(b0, b4, b1, 1.0, (qa, b1), (qa, b4))
        step(b2, b4, b3, 1.0, (qa, b3))
        step(b1, b4, b2, 1.0, (qa, b2))
        step(b3, b1, b1, qc, (qb, b1))
        step(b4, b3, b0, 1.0, (qa, b0), (qa * qa, b3))

        def apply(got, out, block, i, rows):
            x = rows_of(got, block, i).astype(f32)
            y = jnp.dot(b4[rows, :], block_of(got, block), preferred_element_type=f32) + qa**3 * x
            y = (y * scale).reshape(16, 24, got.shape[2])
            out[pl.ds(block * 32 + i * 16, 16)] = y.astype(bf16)

        @pl.when(is_sq)
        def _():
            s = jnp.where(
                u == 2, 32 + (2 * yy + te // 2) * 2 + core, te + 4 * yy + 16 * (u // 2)
            )

            def back(k, carry):
                x, i = lax.rem(k // 2 + te, 4), lax.rem(k, 2)
                apply(got_sq, out_sq, x, i, pl.ds(pl.multiple_of(i * HALF, HALF), HALF))

                def piece(t, c2):
                    r = i * 16 + lax.rem(t + 4 * yy + se, 16)
                    put(
                        out_sq.at[x * 32 + r], up_sq.at[s], 0, send2, recv2, own2,
                        r // 4, x, lax.rem(r, 4),
                    )
                    return c2

                lax.fori_loop(0, 16, piece, 0)
                return carry

            lax.fori_loop(0, 8, back, 0)

        @pl.when(is_wide)
        def _():
            w = wide_of(te, yy, se)

            def back(k, carry):
                x, i = lax.rem(k // 2 + te, 2), lax.rem(k, 2)
                apply(got_wd, out_wd, x, i, pl.ds(pl.multiple_of(i * HALF, HALF), HALF))

                def piece(t, c2):
                    r = i * 16 + lax.rem(t + 4 * yy + se, 16)
                    around = jnp.logical_and(
                        lax.rem(r // 4, 2) == 1, lax.rem(te + 2, 4) == 2 * core + x
                    )

                    @pl.when(around)
                    def _():
                        slot = r // 8 * 4 + lax.rem(r, 4)
                        pltpu.make_async_remote_copy(
                            src_ref=out_wd.at[x * 32 + r], dst_ref=via2.at[slot],
                            send_sem=send2.at[1], recv_sem=recv_v2.at[slot],
                            device_id=(2 * yy + 1, 3 - te, se), device_id_type=MESH,
                        ).start()

                    @pl.when(jnp.logical_not(around))
                    def _():
                        put(
                            out_wd.at[x * 32 + r], up_wd.at[w], 1, send2, recv2, own2,
                            r // 4, 2 * core + x, lax.rem(r, 4),
                        )

                    return c2

                lax.fori_loop(0, 16, piece, 0)
                return carry

            lax.fori_loop(0, 4, back, 0)

    @pl.when(is_sq)
    def _():
        pltpu.make_async_copy(out_sq.at[0], up_sq.at[0], own2.at[0]).wait()
        all_of(st_sq.at[pl.ds(0, 47)], send1, recv1, 0).wait_send()
        all_of(out_sq.at[pl.ds(0, 127)], send2, recv2, 0).wait_send()
        all_of(up_sq.at[pl.ds(0, 47)], send2, recv2, 0).wait_recv()

    @pl.when(jnp.logical_not(is_sq))
    def _():
        all_of(st_sq, send1, recv1, 0).wait_send()
        all_of(up_sq, send2, recv2, 0).wait_recv()

    @pl.when(own_w)
    def _():
        pltpu.make_async_copy(out_wd.at[0], up_wd.at[0], own2.at[1]).wait()
        all_of(st_wd.at[pl.ds(0, 23)], send1, recv1, 1).wait_send()
        all_of(out_wd.at[pl.ds(0, 63)], send2, recv2, 1).wait_send()
        all_of(up_wd.at[pl.ds(0, 23)], send2, recv2, 1).wait_recv()

    @pl.when(jnp.logical_not(own_w))
    def _():
        all_of(st_wd, send1, recv1, 1).wait_send()
        all_of(up_wd, send2, recv2, 1).wait_recv()

    @pl.when(jnp.logical_and(is_wide, jnp.logical_not(own_w)))
    def _():
        all_of(out_wd, send2, recv2, 1).wait_send()


    @pl.when(via_in)
    def _():
        all_of(via1.at[pl.ds(0, 12)], sent_v, recv1, 0).wait_send()

    @pl.when(via_out)
    def _():
        all_of(via2, sent_v, recv1, 1).wait_send()


def orthogonalize(start_sq, start_wd):
    any_space = pl.BlockSpec(memory_space=pl.ANY)
    vmem = pltpu.VMEM
    bf16 = jnp.bfloat16
    pair = pltpu.SemaphoreType.DMA((2,))
    return pl.pallas_call(
        kernel,
        out_shape=(
            jax.ShapeDtypeStruct((48, 24, 192), bf16),
            jax.ShapeDtypeStruct((24, 24, 768), bf16),
        ),
        in_specs=[any_space] * 2,
        out_specs=[any_space] * 2,
        scratch_shapes=[
            vmem((128, 24, 192), bf16), vmem((64, 24, 768), bf16),
            vmem((128, 24, 192), bf16), vmem((64, 24, 768), bf16),
            vmem((16, 24, 768), bf16), vmem((16, 24, 768), bf16), vmem((8, 128), jnp.float32),
            vmem((768, 768), jnp.float32), vmem((768, 768), bf16), vmem((768, 768), bf16),
        ] + [vmem((768, 768), bf16)] * 5 + [pair] * 9 + [pltpu.SemaphoreType.DMA((16,))] * 2,
        compiler_params=pltpu.CompilerParams(collective_id=0, has_side_effects=True),
    )(start_sq, start_wd)


def local(grad_square, grad_wide, momentum_square, momentum_wide, weights_square, weights_wide):
    moment_sq = momentum_beta * momentum_square + grad_square.astype(jnp.float32)
    moment_wd = momentum_beta * momentum_wide + grad_wide.astype(jnp.float32)
    start_sq = (grad_square.astype(jnp.float32) + momentum_beta * moment_sq).astype(jnp.bfloat16)
    start_wd = (grad_wide.astype(jnp.float32) + momentum_beta * moment_wd).astype(jnp.bfloat16)
    done_sq, done_wd = orthogonalize(
        start_sq.reshape(48, 24, 192), start_wd.reshape(24, 24, 768)
    )
    done_sq = done_sq.reshape(start_sq.shape).astype(jnp.float32)
    done_wd = done_wd.reshape(start_wd.shape).astype(jnp.float32)
    update_sq = (0.2 * math.sqrt(768) * done_sq).astype(jnp.bfloat16)
    update_wd = (0.2 * math.sqrt(3072) * done_wd).astype(jnp.bfloat16)
    keep = 1.0 - learning_rate * weight_decay
    weight_sq = weights_square * keep - learning_rate * update_sq.astype(jnp.float32)
    weight_wd = weights_wide * keep - learning_rate * update_wd.astype(jnp.float32)
    return (moment_sq, moment_wd, update_sq, update_wd, weight_sq, weight_wd)


def solution(mesh):
    spec = P(None, None, ("shard", "section"), "tensor")
    return jax.shard_map(
        local, mesh=mesh, in_specs=(spec,) * 6, out_specs=(spec,) * 6, check_vma=False
    )
```

```python
import math

import jax
import jax.numpy as jnp
from jax import lax
from jax.experimental import pallas as pl
from jax.experimental.pallas import tpu as pltpu
from jax.sharding import PartitionSpec as P

momentum_beta = 0.95
norm_epsilon = 1e-07
learning_rate = 0.02
weight_decay = 0.01
qa = 3.4445
qb = -4.775
qc = 2.0315

MESH = pl.DeviceIdType.MESH
HALF = 384


def kernel(
    st_sq, st_wd, up_sq, up_wd,
    got_sq, got_wd, out_sq, out_wd, via1, via2, trace, g32, part_out, part_in, b0, b1, b2, b3, b4,
    send1, recv1, own1, send2, recv2, own2, send_p, recv_p, sent_v, recv_v1, recv_v2,
):
    sh, te, se = lax.axis_index("shard"), lax.axis_index("tensor"), lax.axis_index("section")
    core, yy = lax.rem(sh, 2), sh // 2
    row = sh * 4 + se
    f32, bf16 = jnp.float32, jnp.bfloat16

    barrier = pltpu.get_barrier_semaphore()
    for i in range(1, 128):
        a, b, c = i // 16, (i // 4) % 4, i % 4
        pl.semaphore_signal(
            barrier, inc=1,
            device_id=(lax.rem(sh + a, 8), lax.rem(te + b, 4), lax.rem(se + c, 4)),
            device_id_type=MESH,
        )
    pl.semaphore_wait(barrier, 127)

    u = lax.rem(se - te - yy + 8, 4)
    odd = lax.rem(te + yy, 2)
    is_wide = jnp.logical_or(u == 0, jnp.logical_and(u == 2, odd == 0))
    is_sq = jnp.logical_or(
        jnp.logical_and(lax.rem(u, 2) == 1, core == 0), jnp.logical_and(u == 2, odd == 1)
    )
    own_w = jnp.logical_and(is_wide, te // 2 == core)
    near_z = se + 1 - 2 * lax.rem(se, 2)

    def wide_at(x, y, z):
        v = lax.rem(z - x - y + 8, 4)
        return jnp.logical_or(v == 0, jnp.logical_and(v == 2, lax.rem(x + y, 2) == 0))

    def wide_of(x, y, z):
        v = lax.rem(z - x - y + 8, 4)
        return (1 - v // 2) * (x + 4 * y) + (v // 2) * (16 + 2 * y + x // 2)

    spare = jnp.logical_and(lax.rem(u, 2) == 1, core == 1)
    via_in = jnp.logical_and(spare, wide_at(te, yy, near_z))
    via_out = jnp.logical_and(spare, wide_at(3 - te, yy, se))

    def put(src, dst, k, send, recv, own, dsh, dte, dse):
        mine = jnp.logical_and(jnp.logical_and(dsh == sh, dte == te), dse == se)

        @pl.when(mine)
        def _():
            pltpu.make_async_copy(src, dst, own.at[k]).start()

        @pl.when(jnp.logical_not(mine))
        def _():
            pltpu.make_async_remote_copy(
                src_ref=src, dst_ref=dst, send_sem=send.at[k], recv_sem=recv.at[k],
                device_id=(dsh, dte, dse), device_id_type=MESH,
            ).start()

    def all_of(ref, send, recv, k):
        return pltpu.make_async_remote_copy(
            src_ref=ref, dst_ref=ref, send_sem=send.at[k], recv_sem=recv.at[k],
            device_id=(sh, te, se), device_id_type=MESH,
        )

    def line(e):
        return lax.rem(te + lax.rem(e, 4), 4), lax.rem(yy + e // 4, 4)

    def line_of(l, parity):
        y = lax.rem(yy + l // 2, 4)
        return lax.rem(2 * lax.rem(l, 2) + te + lax.rem(te + y + parity, 2), 4), y

    def wide_to(xy, late):
        x, y = xy
        w = 16 + 2 * y + x // 2 if late else x + 4 * y
        z = lax.rem(x + y + 2 * late, 4)
        around = jnp.logical_and(jnp.logical_and(core == 1, yy < 3), lax.rem(z + 2, 4) == se)

        @pl.when(around)
        def _():
            slot = te * 3 + yy
            pltpu.make_async_remote_copy(
                src_ref=st_wd.at[w], dst_ref=via1.at[slot],
                send_sem=send1.at[1], recv_sem=recv_v1.at[slot],
                device_id=(2 * y + 1, x, z + 1 - 2 * lax.rem(z, 2)), device_id_type=MESH,
            ).start()

        @pl.when(jnp.logical_not(around))
        def _():
            put(
                st_wd.at[w], got_wd.at[lax.rem(te, 2) * 32 + row], 1, send1, recv1, own1,
                y * 2 + te // 2, x, z,
            )

    def square_to(xy, g, c):
        x, y = xy
        s = 32 + (2 * y + x // 2) * 2 + c if g == 2 else x + 4 * y + 16 * g
        put(
            st_sq.at[s], got_sq.at[te * 32 + row], 0, send1, recv1, own1,
            y * 2 + c, x, lax.rem(x + y + (1, 3, 2)[g], 4),
        )

    def send_wides(i, carry):
        q = lax.rem(i + 2 * se + 4 * core, 8)
        wide_to(line(2 * q), 0)
        wide_to(line(2 * q + 1), 0)
        wide_to(line_of(lax.rem(q + 3, 8), 0), 1)
        return carry

    def send_squares(i, carry):
        q = lax.rem(i + 2 * se + 4 * core, 8)
        for j in range(2):
            square_to(line(2 * q + j), 0, 0)
            square_to(line(lax.rem(2 * q + j + 8, 16)), 1, 0)
            square_to(line_of(q, 1), 2, lax.rem(j + core, 2))
        return carry

    lax.fori_loop(0, 8, send_wides, 0)

    @pl.when(via_in)
    def _():
        def onward(slot, carry):
            x = slot // 3
            far_row = (2 * lax.rem(slot, 3) + 1) * 4 + lax.rem(near_z + 2, 4)
            copy = pltpu.make_async_remote_copy(
                src_ref=via1.at[slot], dst_ref=via1.at[slot],
                send_sem=sent_v.at[0], recv_sem=recv_v1.at[slot],
                device_id=(sh, te, se), device_id_type=MESH,
            )
            copy.wait_recv()
            pltpu.make_async_remote_copy(
                src_ref=via1.at[slot], dst_ref=got_wd.at[lax.rem(x, 2) * 32 + far_row],
                send_sem=sent_v.at[0], recv_sem=recv1.at[1],
                device_id=(2 * yy + x // 2, te, near_z), device_id_type=MESH,
            ).start()
            return carry

        lax.fori_loop(0, 12, onward, 0)

    lax.fori_loop(0, 8, send_squares, 0)

    @pl.when(via_out)
    def _():
        w_far = wide_of(3 - te, yy, se)

        def onward(t, carry):
            r = t // 16 * 16 + lax.rem(t + 4 * yy + se, 16)

            @pl.when(lax.rem(r // 4, 2) == 1)
            def _():
                slot = r // 8 * 4 + lax.rem(r, 4)
                copy = pltpu.make_async_remote_copy(
                    src_ref=via2.at[slot], dst_ref=via2.at[slot],
                    send_sem=sent_v.at[1], recv_sem=recv_v2.at[slot],
                    device_id=(sh, te, se), device_id_type=MESH,
                )
                copy.wait_recv()
                pltpu.make_async_remote_copy(
                    src_ref=via2.at[slot], dst_ref=up_wd.at[w_far],
                    send_sem=sent_v.at[1], recv_sem=recv2.at[1],
                    device_id=(r // 4, lax.rem(5 - te, 4), lax.rem(r, 4)),
                    device_id_type=MESH,
                ).start()

            return carry

        lax.fori_loop(0, 32, onward, 0)

    def halves(body, init=0):
        def one(i, carry):
            return body(i, pl.ds(pl.multiple_of(i * HALF, HALF), HALF), carry)

        return lax.fori_loop(0, 2, one, init)

    def diag_sum(i, block):
        r = lax.broadcasted_iota(jnp.int32, block.shape, 0) + i * HALF
        c = lax.broadcasted_iota(jnp.int32, block.shape, 1)
        return jnp.sum(jnp.where(r == c, block, 0.0), keepdims=True)

    def flip(a, b):
        return lax.dot_general(a, b, (((1,), (1,)), ((), ())), preferred_element_type=f32)

    def rows_of(ref, j, i):
        return ref[pl.ds(j * 32 + i * 16, 16)].reshape(HALF, ref.shape[2])

    def block_of(ref, j):
        return ref[pl.ds(j * 32, 32)].reshape(768, ref.shape[2])

    top, low = slice(0, HALF), slice(HALF, 768)
    quarters = ((0, top, top), (1, top, low), (2, low, low))

    def quarter(got, blocks, k):
        i, j = k // 2, (k + 1) // 2
        total = flip(rows_of(got, 0, i), rows_of(got, 0, j))
        for x in range(1, blocks):
            total += flip(rows_of(got, x, i), rows_of(got, x, j))
        return total

    def keep(k, rows, cols, total):
        block = total.astype(bf16)
        b0[rows, cols] = block
        if k == 1:
            b0[cols, rows] = block.T
        else:
            trace[...] += jnp.broadcast_to(diag_sum(0, total), trace.shape)

    @pl.when(jnp.logical_or(is_sq, is_wide))
    def _():
        trace[...] = jnp.zeros_like(trace)

    @pl.when(is_sq)
    def _():
        pltpu.make_async_copy(st_sq.at[0], got_sq.at[0], own1.at[0]).wait()
        all_of(got_sq.at[pl.ds(0, 127)], send1, recv1, 0).wait_recv()
        for k, rows, cols in quarters:
            keep(k, rows, cols, quarter(got_sq, 4, k))

    @pl.when(is_wide)
    def _():
        @pl.when(own_w)
        def _():
            pltpu.make_async_copy(st_wd.at[0], got_wd.at[0], own1.at[1]).wait()
            all_of(got_wd.at[pl.ds(0, 63)], send1, recv1, 1).wait_recv()

        @pl.when(jnp.logical_not(own_w))
        def _():
            all_of(got_wd, send1, recv1, 1).wait_recv()

        def swap(k):
            return pltpu.make_async_remote_copy(
                src_ref=part_out.at[k], dst_ref=part_in.at[k],
                send_sem=send_p.at[k], recv_sem=recv_p.at[k],
                device_id=(sh + 1 - 2 * core, te, se), device_id_type=MESH,
            )

        for k, rows, cols in quarters:
            total = quarter(got_wd, 2, k)
            g32[k] = total
            part_out[k] = total.astype(bf16)
            swap(k).start()
        for k, rows, cols in quarters:
            swap(k).wait()
            keep(k, rows, cols, g32[k] + part_in[k].astype(f32))

    def step(dst, left, right, gain, *terms):
        def part(rows, cols):
            y = gain * jnp.dot(left[rows, :], right[:, cols], preferred_element_type=f32)
            for weight, term in terms:
                y += weight * term[rows, cols].astype(f32)
            return y.astype(bf16)

        upper = part(top, slice(0, 768))
        dst[top, :] = upper
        dst[low, top] = upper[:, HALF:].T
        dst[low, low] = part(low, low)

    @pl.when(jnp.logical_or(is_sq, is_wide))
    def _():
        scale = 1.0 / (jnp.sqrt(trace[0:1, 0:1]) + norm_epsilon)
        gain = scale * scale
        step(b1, b0, b0, qc * gain * gain, (qb * gain, b0))
        step(b2, b1, b0, gain, (qa * gain, b0))
        step(b3, b1, b2, 1.0, (qa, b2))
        step(b4, b3, b3, qc, (qb, b3))
        step(b0, b4, b1, 1.0, (qa, b1), (qa, b4))
        step(b2, b4, b3, 1.0, (qa, b3))
        step(b1, b4, b2, 1.0, (qa, b2))
        step(b3, b1, b1, qc, (qb, b1))
        step(b4, b3, b0, 1.0, (qa, b0), (qa * qa, b3))

        def apply(got, out, block, i, rows):
            x = rows_of(got, block, i).astype(f32)
            y = jnp.dot(b4[rows, :], block_of(got, block), preferred_element_type=f32) + qa**3 * x
            y = (y * scale).reshape(16, 24, got.shape[2])
            out[pl.ds(block * 32 + i * 16, 16)] = y.astype(bf16)

        @pl.when(is_sq)
        def _():
            s = jnp.where(
                u == 2, 32 + (2 * yy + te // 2) * 2 + core, te + 4 * yy + 16 * (u // 2)
            )

            def back(k, carry):
                x, i = lax.rem(k // 2 + te, 4), lax.rem(k, 2)
                apply(got_sq, out_sq, x, i, pl.ds(pl.multiple_of(i * HALF, HALF), HALF))

                def piece(t, c2):
                    r = i * 16 + lax.rem(t + 4 * yy + se, 16)
                    put(
                        out_sq.at[x * 32 + r], up_sq.at[s], 0, send2, recv2, own2,
                        r // 4, x, lax.rem(r, 4),
                    )
                    return c2

                lax.fori_loop(0, 16, piece, 0)
                return carry

            lax.fori_loop(0, 8, back, 0)

        @pl.when(is_wide)
        def _():
            w = wide_of(te, yy, se)

            def back(k, carry):
                x, i = lax.rem(k // 2 + te, 2), lax.rem(k, 2)
                apply(got_wd, out_wd, x, i, pl.ds(pl.multiple_of(i * HALF, HALF), HALF))

                def piece(t, c2):
                    r = i * 16 + lax.rem(t + 4 * yy + se, 16)
                    around = jnp.logical_and(
                        lax.rem(r // 4, 2) == 1, lax.rem(te + 2, 4) == 2 * core + x
                    )

                    @pl.when(around)
                    def _():
                        slot = r // 8 * 4 + lax.rem(r, 4)
                        pltpu.make_async_remote_copy(
                            src_ref=out_wd.at[x * 32 + r], dst_ref=via2.at[slot],
                            send_sem=send2.at[1], recv_sem=recv_v2.at[slot],
                            device_id=(2 * yy + 1, 3 - te, se), device_id_type=MESH,
                        ).start()

                    @pl.when(jnp.logical_not(around))
                    def _():
                        put(
                            out_wd.at[x * 32 + r], up_wd.at[w], 1, send2, recv2, own2,
                            r // 4, 2 * core + x, lax.rem(r, 4),
                        )

                    return c2

                lax.fori_loop(0, 16, piece, 0)
                return carry

            lax.fori_loop(0, 4, back, 0)

    @pl.when(is_sq)
    def _():
        pltpu.make_async_copy(out_sq.at[0], up_sq.at[0], own2.at[0]).wait()
        all_of(st_sq.at[pl.ds(0, 47)], send1, recv1, 0).wait_send()
        all_of(out_sq.at[pl.ds(0, 127)], send2, recv2, 0).wait_send()
        all_of(up_sq.at[pl.ds(0, 47)], send2, recv2, 0).wait_recv()

    @pl.when(jnp.logical_not(is_sq))
    def _():
        all_of(st_sq, send1, recv1, 0).wait_send()
        all_of(up_sq, send2, recv2, 0).wait_recv()

    @pl.when(own_w)
    def _():
        pltpu.make_async_copy(out_wd.at[0], up_wd.at[0], own2.at[1]).wait()
        all_of(st_wd.at[pl.ds(0, 23)], send1, recv1, 1).wait_send()
        all_of(out_wd.at[pl.ds(0, 63)], send2, recv2, 1).wait_send()
        all_of(up_wd.at[pl.ds(0, 23)], send2, recv2, 1).wait_recv()

    @pl.when(jnp.logical_not(own_w))
    def _():
        all_of(st_wd, send1, recv1, 1).wait_send()
        all_of(up_wd, send2, recv2, 1).wait_recv()

    @pl.when(jnp.logical_and(is_wide, jnp.logical_not(own_w)))
    def _():
        all_of(out_wd, send2, recv2, 1).wait_send()


    @pl.when(via_in)
    def _():
        all_of(via1.at[pl.ds(0, 12)], sent_v, recv1, 0).wait_send()

    @pl.when(via_out)
    def _():
        all_of(via2, sent_v, recv1, 1).wait_send()


def orthogonalize(start_sq, start_wd):
    any_space = pl.BlockSpec(memory_space=pl.ANY)
    vmem = pltpu.VMEM
    bf16 = jnp.bfloat16
    pair = pltpu.SemaphoreType.DMA((2,))
    return pl.pallas_call(
        kernel,
        out_shape=(
            jax.ShapeDtypeStruct((48, 24, 192), bf16),
            jax.ShapeDtypeStruct((24, 24, 768), bf16),
        ),
        in_specs=[any_space] * 2,
        out_specs=[any_space] * 2,
        scratch_shapes=[
            vmem((128, 24, 192), bf16), vmem((64, 24, 768), bf16),
            vmem((128, 24, 192), bf16), vmem((64, 24, 768), bf16),
            vmem((16, 24, 768), bf16), vmem((16, 24, 768), bf16), vmem((8, 128), jnp.float32),
            vmem((3, HALF, HALF), jnp.float32), vmem((3, HALF, HALF), bf16), vmem((3, HALF, HALF), bf16),
        ] + [vmem((768, 768), bf16)] * 5 + [pair] * 6 + [pltpu.SemaphoreType.DMA((3,))] * 2 + [pair] + [pltpu.SemaphoreType.DMA((16,))] * 2,
        compiler_params=pltpu.CompilerParams(collective_id=0, has_side_effects=True, vmem_limit_bytes=32 * 1024 * 1024),
    )(start_sq, start_wd)


def local(grad_square, grad_wide, momentum_square, momentum_wide, weights_square, weights_wide):
    moment_sq = momentum_beta * momentum_square + grad_square.astype(jnp.float32)
    moment_wd = momentum_beta * momentum_wide + grad_wide.astype(jnp.float32)
    start_sq = (grad_square.astype(jnp.float32) + momentum_beta * moment_sq).astype(jnp.bfloat16)
    start_wd = (grad_wide.astype(jnp.float32) + momentum_beta * moment_wd).astype(jnp.bfloat16)
    done_sq, done_wd = orthogonalize(
        start_sq.reshape(48, 24, 192), start_wd.reshape(24, 24, 768)
    )
    done_sq = done_sq.reshape(start_sq.shape).astype(jnp.float32)
    done_wd = done_wd.reshape(start_wd.shape).astype(jnp.float32)
    update_sq = (0.2 * math.sqrt(768) * done_sq).astype(jnp.bfloat16)
    update_wd = (0.2 * math.sqrt(3072) * done_wd).astype(jnp.bfloat16)
    keep = 1.0 - learning_rate * weight_decay
    weight_sq = weights_square * keep - learning_rate * update_sq.astype(jnp.float32)
    weight_wd = weights_wide * keep - learning_rate * update_wd.astype(jnp.float32)
    return (moment_sq, moment_wd, update_sq, update_wd, weight_sq, weight_wd)


def solution(mesh):
    spec = P(None, None, ("shard", "section"), "tensor")
    return jax.shard_map(
        local, mesh=mesh, in_specs=(spec,) * 6, out_specs=(spec,) * 6, check_vma=False
    )
```

```python
import math

import jax
import jax.numpy as jnp
from jax import lax
from jax.experimental import pallas as pl
from jax.experimental.pallas import tpu as pltpu
from jax.sharding import PartitionSpec as P

momentum_beta = 0.95
norm_epsilon = 1e-07
learning_rate = 0.02
weight_decay = 0.01
qa = 3.4445
qb = -4.775
qc = 2.0315

MESH = pl.DeviceIdType.MESH
HALF = 384


def kernel(
    st_sq, st_wd, up_sq, up_wd,
    got_sq, got_wd, out_sq, out_wd, via1, via2, trace, g32, part_out, part_in, b0, b1, b2, b3, b4,
    send1, recv1, own1, send2, recv2, own2, send_p, recv_p, sent_v, recv_v1, recv_v2,
):
    sh, te, se = lax.axis_index("shard"), lax.axis_index("tensor"), lax.axis_index("section")
    core, yy = lax.rem(sh, 2), sh // 2
    row = sh * 4 + se
    f32, bf16 = jnp.float32, jnp.bfloat16

    barrier = pltpu.get_barrier_semaphore()
    for i in range(1, 128):
        a, b, c = i // 16, (i // 4) % 4, i % 4
        pl.semaphore_signal(
            barrier, inc=1,
            device_id=(lax.rem(sh + a, 8), lax.rem(te + b, 4), lax.rem(se + c, 4)),
            device_id_type=MESH,
        )
    pl.semaphore_wait(barrier, 127)

    u = lax.rem(se - te - yy + 8, 4)
    odd = lax.rem(te + yy, 2)
    is_wide = jnp.logical_or(u == 0, jnp.logical_and(u == 2, odd == 0))
    is_sq = jnp.logical_or(
        jnp.logical_and(lax.rem(u, 2) == 1, core == 0), jnp.logical_and(u == 2, odd == 1)
    )
    own_w = jnp.logical_and(is_wide, te // 2 == core)
    near_z = se + 1 - 2 * lax.rem(se, 2)

    def wide_at(x, y, z):
        v = lax.rem(z - x - y + 8, 4)
        return jnp.logical_or(v == 0, jnp.logical_and(v == 2, lax.rem(x + y, 2) == 0))

    def wide_of(x, y, z):
        v = lax.rem(z - x - y + 8, 4)
        return (1 - v // 2) * (x + 4 * y) + (v // 2) * (16 + 2 * y + x // 2)

    spare = jnp.logical_and(lax.rem(u, 2) == 1, core == 1)
    via_in = jnp.logical_and(spare, wide_at(te, yy, near_z))
    via_out = jnp.logical_and(spare, wide_at(3 - te, yy, se))

    def put(src, dst, k, send, recv, own, dsh, dte, dse):
        mine = jnp.logical_and(jnp.logical_and(dsh == sh, dte == te), dse == se)

        @pl.when(mine)
        def _():
            pltpu.make_async_copy(src, dst, own.at[k]).start()

        @pl.when(jnp.logical_not(mine))
        def _():
            pltpu.make_async_remote_copy(
                src_ref=src, dst_ref=dst, send_sem=send.at[k], recv_sem=recv.at[k],
                device_id=(dsh, dte, dse), device_id_type=MESH,
            ).start()

    def all_of(ref, send, recv, k):
        return pltpu.make_async_remote_copy(
            src_ref=ref, dst_ref=ref, send_sem=send.at[k], recv_sem=recv.at[k],
            device_id=(sh, te, se), device_id_type=MESH,
        )

    def line(e):
        return lax.rem(te + lax.rem(e, 4), 4), lax.rem(yy + e // 4, 4)

    def line_of(l, parity):
        y = lax.rem(yy + l // 2, 4)
        return lax.rem(2 * lax.rem(l, 2) + te + lax.rem(te + y + parity, 2), 4), y

    def wide_to(xy, late):
        x, y = xy
        w = 16 + 2 * y + x // 2 if late else x + 4 * y
        z = lax.rem(x + y + 2 * late, 4)
        around = jnp.logical_and(jnp.logical_and(core == 1, yy < 3), lax.rem(z + 2, 4) == se)

        @pl.when(around)
        def _():
            slot = te * 3 + yy
            pltpu.make_async_remote_copy(
                src_ref=st_wd.at[w], dst_ref=via1.at[slot],
                send_sem=send1.at[1], recv_sem=recv_v1.at[slot],
                device_id=(2 * y + 1, x, z + 1 - 2 * lax.rem(z, 2)), device_id_type=MESH,
            ).start()

        @pl.when(jnp.logical_not(around))
        def _():
            put(
                st_wd.at[w], got_wd.at[lax.rem(te, 2) * 32 + row], 1, send1, recv1, own1,
                y * 2 + te // 2, x, z,
            )

    def square_to(xy, g, c):
        x, y = xy
        s = 32 + (2 * y + x // 2) * 2 + c if g == 2 else x + 4 * y + 16 * g
        put(
            st_sq.at[s], got_sq.at[te * 32 + row], 0, send1, recv1, own1,
            y * 2 + c, x, lax.rem(x + y + (1, 3, 2)[g], 4),
        )

    def send_wides(i, carry):
        q = lax.rem(i + 2 * se + 4 * core, 8)
        wide_to(line(2 * q), 0)
        wide_to(line(2 * q + 1), 0)
        wide_to(line_of(lax.rem(q + 3, 8), 0), 1)
        return carry

    def send_squares(i, carry):
        q = lax.rem(i + 2 * se + 4 * core, 8)
        for j in range(2):
            square_to(line(2 * q + j), 0, 0)
            square_to(line(lax.rem(2 * q + j + 8, 16)), 1, 0)
            square_to(line_of(q, 1), 2, lax.rem(j + core, 2))
        return carry

    lax.fori_loop(0, 8, send_wides, 0)

    @pl.when(via_in)
    def _():
        def onward(slot, carry):
            x = slot // 3
            far_row = (2 * lax.rem(slot, 3) + 1) * 4 + lax.rem(near_z + 2, 4)
            copy = pltpu.make_async_remote_copy(
                src_ref=via1.at[slot], dst_ref=via1.at[slot],
                send_sem=sent_v.at[0], recv_sem=recv_v1.at[slot],
                device_id=(sh, te, se), device_id_type=MESH,
            )
            copy.wait_recv()
            pltpu.make_async_remote_copy(
                src_ref=via1.at[slot], dst_ref=got_wd.at[lax.rem(x, 2) * 32 + far_row],
                send_sem=sent_v.at[0], recv_sem=recv1.at[1],
                device_id=(2 * yy + x // 2, te, near_z), device_id_type=MESH,
            ).start()
            return carry

        lax.fori_loop(0, 12, onward, 0)

    lax.fori_loop(0, 8, send_squares, 0)

    @pl.when(via_out)
    def _():
        w_far = wide_of(3 - te, yy, se)

        def onward(t, carry):
            r = t // 16 * 16 + lax.rem(t + 4 * yy + se, 16)

            @pl.when(lax.rem(r // 4, 2) == 1)
            def _():
                slot = r // 8 * 4 + lax.rem(r, 4)
                copy = pltpu.make_async_remote_copy(
                    src_ref=via2.at[slot], dst_ref=via2.at[slot],
                    send_sem=sent_v.at[1], recv_sem=recv_v2.at[slot],
                    device_id=(sh, te, se), device_id_type=MESH,
                )
                copy.wait_recv()
                pltpu.make_async_remote_copy(
                    src_ref=via2.at[slot], dst_ref=up_wd.at[w_far],
                    send_sem=sent_v.at[1], recv_sem=recv2.at[1],
                    device_id=(r // 4, lax.rem(5 - te, 4), lax.rem(r, 4)),
                    device_id_type=MESH,
                ).start()

            return carry

        lax.fori_loop(0, 32, onward, 0)

    def halves(body, init=0):
        def one(i, carry):
            return body(i, pl.ds(pl.multiple_of(i * HALF, HALF), HALF), carry)

        return lax.fori_loop(0, 2, one, init)

    def diag_sum(i, block):
        r = lax.broadcasted_iota(jnp.int32, block.shape, 0) + i * HALF
        c = lax.broadcasted_iota(jnp.int32, block.shape, 1)
        return jnp.sum(jnp.where(r == c, block, 0.0), keepdims=True)

    def flip(a, b):
        return lax.dot_general(a, b, (((1,), (1,)), ((), ())), preferred_element_type=f32)

    def rows_of(ref, j, i):
        return ref[pl.ds(j * 32 + i * 16, 16)].reshape(HALF, ref.shape[2])

    def block_of(ref, j):
        return ref[pl.ds(j * 32, 32)].reshape(768, ref.shape[2])

    top, low = slice(0, HALF), slice(HALF, 768)
    quarters = ((0, top, top), (1, top, low), (2, low, low))

    def quarter(got, blocks, k):
        i, j = k // 2, (k + 1) // 2
        total = flip(rows_of(got, 0, i), rows_of(got, 0, j))
        for x in range(1, blocks):
            total += flip(rows_of(got, x, i), rows_of(got, x, j))
        return total

    def keep(k, rows, cols, total):
        block = total.astype(bf16)
        b0[rows, cols] = block
        if k == 1:
            b0[cols, rows] = block.T
        else:
            trace[...] += jnp.broadcast_to(diag_sum(0, total), trace.shape)

    @pl.when(jnp.logical_or(is_sq, is_wide))
    def _():
        trace[...] = jnp.zeros_like(trace)

    @pl.when(is_sq)
    def _():
        pltpu.make_async_copy(st_sq.at[0], got_sq.at[0], own1.at[0]).wait()
        all_of(got_sq.at[pl.ds(0, 127)], send1, recv1, 0).wait_recv()
        for k, rows, cols in quarters:
            keep(k, rows, cols, quarter(got_sq, 4, k))

    @pl.when(is_wide)
    def _():
        @pl.when(own_w)
        def _():
            pltpu.make_async_copy(st_wd.at[0], got_wd.at[0], own1.at[1]).wait()
            all_of(got_wd.at[pl.ds(0, 63)], send1, recv1, 1).wait_recv()

        @pl.when(jnp.logical_not(own_w))
        def _():
            all_of(got_wd, send1, recv1, 1).wait_recv()

        def swap(k):
            return pltpu.make_async_remote_copy(
                src_ref=part_out.at[k], dst_ref=part_in.at[k],
                send_sem=send_p.at[k], recv_sem=recv_p.at[k],
                device_id=(sh + 1 - 2 * core, te, se), device_id_type=MESH,
            )

        for k, rows, cols in quarters:
            total = quarter(got_wd, 2, k)
            g32[k] = total
            part_out[k] = total.astype(bf16)
            swap(k).start()
        for k, rows, cols in quarters:
            swap(k).wait()
            keep(k, rows, cols, g32[k] + part_in[k].astype(f32))

    def step(dst, left, right, gain, *terms):
        def part(rows, cols):
            y = gain * jnp.dot(left[rows, :], right[:, cols], preferred_element_type=f32)
            for weight, term in terms:
                y += weight * term[rows, cols].astype(f32)
            return y.astype(bf16)

        for first in range(0, 768, 256):
            rows = slice(first, first + 256)
            upper = part(rows, slice(first, 768))
            dst[rows, first:] = upper
            if first < 512:
                dst[first + 256 :, rows] = upper[:, 256:].T

    @pl.when(jnp.logical_or(is_sq, is_wide))
    def _():
        scale = 1.0 / (jnp.sqrt(trace[0:1, 0:1]) + norm_epsilon)
        gain = scale * scale
        step(b1, b0, b0, qc * gain * gain, (qb * gain, b0))
        step(b2, b1, b0, gain, (qa * gain, b0))
        step(b3, b1, b2, 1.0, (qa, b2))
        step(b4, b3, b3, qc, (qb, b3))
        step(b0, b4, b1, 1.0, (qa, b1), (qa, b4))
        step(b2, b4, b3, 1.0, (qa, b3))
        step(b1, b4, b2, 1.0, (qa, b2))
        step(b3, b1, b1, qc, (qb, b1))
        step(b4, b3, b0, 1.0, (qa, b0), (qa * qa, b3))

        def apply(got, out, block, i, rows):
            x = rows_of(got, block, i).astype(f32)
            y = jnp.dot(b4[rows, :], block_of(got, block), preferred_element_type=f32) + qa**3 * x
            y = (y * scale).reshape(16, 24, got.shape[2])
            out[pl.ds(block * 32 + i * 16, 16)] = y.astype(bf16)

        @pl.when(is_sq)
        def _():
            s = jnp.where(
                u == 2, 32 + (2 * yy + te // 2) * 2 + core, te + 4 * yy + 16 * (u // 2)
            )

            def back(k, carry):
                x, i = lax.rem(k // 2 + te, 4), lax.rem(k, 2)
                apply(got_sq, out_sq, x, i, pl.ds(pl.multiple_of(i * HALF, HALF), HALF))

                def piece(t, c2):
                    r = i * 16 + lax.rem(t + 4 * yy + se, 16)
                    put(
                        out_sq.at[x * 32 + r], up_sq.at[s], 0, send2, recv2, own2,
                        r // 4, x, lax.rem(r, 4),
                    )
                    return c2

                lax.fori_loop(0, 16, piece, 0)
                return carry

            lax.fori_loop(0, 8, back, 0)

        @pl.when(is_wide)
        def _():
            w = wide_of(te, yy, se)

            def back(k, carry):
                x, i = lax.rem(k // 2 + te, 2), lax.rem(k, 2)
                apply(got_wd, out_wd, x, i, pl.ds(pl.multiple_of(i * HALF, HALF), HALF))

                def piece(t, c2):
                    r = i * 16 + lax.rem(t + 4 * yy + se, 16)
                    around = jnp.logical_and(
                        lax.rem(r // 4, 2) == 1, lax.rem(te + 2, 4) == 2 * core + x
                    )

                    @pl.when(around)
                    def _():
                        slot = r // 8 * 4 + lax.rem(r, 4)
                        pltpu.make_async_remote_copy(
                            src_ref=out_wd.at[x * 32 + r], dst_ref=via2.at[slot],
                            send_sem=send2.at[1], recv_sem=recv_v2.at[slot],
                            device_id=(2 * yy + 1, 3 - te, se), device_id_type=MESH,
                        ).start()

                    @pl.when(jnp.logical_not(around))
                    def _():
                        put(
                            out_wd.at[x * 32 + r], up_wd.at[w], 1, send2, recv2, own2,
                            r // 4, 2 * core + x, lax.rem(r, 4),
                        )

                    return c2

                lax.fori_loop(0, 16, piece, 0)
                return carry

            lax.fori_loop(0, 4, back, 0)

    @pl.when(is_sq)
    def _():
        pltpu.make_async_copy(out_sq.at[0], up_sq.at[0], own2.at[0]).wait()
        all_of(st_sq.at[pl.ds(0, 47)], send1, recv1, 0).wait_send()
        all_of(out_sq.at[pl.ds(0, 127)], send2, recv2, 0).wait_send()
        all_of(up_sq.at[pl.ds(0, 47)], send2, recv2, 0).wait_recv()

    @pl.when(jnp.logical_not(is_sq))
    def _():
        all_of(st_sq, send1, recv1, 0).wait_send()
        all_of(up_sq, send2, recv2, 0).wait_recv()

    @pl.when(own_w)
    def _():
        pltpu.make_async_copy(out_wd.at[0], up_wd.at[0], own2.at[1]).wait()
        all_of(st_wd.at[pl.ds(0, 23)], send1, recv1, 1).wait_send()
        all_of(out_wd.at[pl.ds(0, 63)], send2, recv2, 1).wait_send()
        all_of(up_wd.at[pl.ds(0, 23)], send2, recv2, 1).wait_recv()

    @pl.when(jnp.logical_not(own_w))
    def _():
        all_of(st_wd, send1, recv1, 1).wait_send()
        all_of(up_wd, send2, recv2, 1).wait_recv()

    @pl.when(jnp.logical_and(is_wide, jnp.logical_not(own_w)))
    def _():
        all_of(out_wd, send2, recv2, 1).wait_send()


    @pl.when(via_in)
    def _():
        all_of(via1.at[pl.ds(0, 12)], sent_v, recv1, 0).wait_send()

    @pl.when(via_out)
    def _():
        all_of(via2, sent_v, recv1, 1).wait_send()


def orthogonalize(start_sq, start_wd):
    any_space = pl.BlockSpec(memory_space=pl.ANY)
    vmem = pltpu.VMEM
    bf16 = jnp.bfloat16
    pair = pltpu.SemaphoreType.DMA((2,))
    return pl.pallas_call(
        kernel,
        out_shape=(
            jax.ShapeDtypeStruct((48, 24, 192), bf16),
            jax.ShapeDtypeStruct((24, 24, 768), bf16),
        ),
        in_specs=[any_space] * 2,
        out_specs=[any_space] * 2,
        scratch_shapes=[
            vmem((128, 24, 192), bf16), vmem((64, 24, 768), bf16),
            vmem((128, 24, 192), bf16), vmem((64, 24, 768), bf16),
            vmem((16, 24, 768), bf16), vmem((16, 24, 768), bf16), vmem((8, 128), jnp.float32),
            vmem((3, HALF, HALF), jnp.float32), vmem((3, HALF, HALF), bf16), vmem((3, HALF, HALF), bf16),
        ] + [vmem((768, 768), bf16)] * 5 + [pair] * 6 + [pltpu.SemaphoreType.DMA((3,))] * 2 + [pair] + [pltpu.SemaphoreType.DMA((16,))] * 2,
        compiler_params=pltpu.CompilerParams(collective_id=0, has_side_effects=True, vmem_limit_bytes=32 * 1024 * 1024),
    )(start_sq, start_wd)


def local(grad_square, grad_wide, momentum_square, momentum_wide, weights_square, weights_wide):
    moment_sq = momentum_beta * momentum_square + grad_square.astype(jnp.float32)
    moment_wd = momentum_beta * momentum_wide + grad_wide.astype(jnp.float32)
    start_sq = (grad_square.astype(jnp.float32) + momentum_beta * moment_sq).astype(jnp.bfloat16)
    start_wd = (grad_wide.astype(jnp.float32) + momentum_beta * moment_wd).astype(jnp.bfloat16)
    done_sq, done_wd = orthogonalize(
        start_sq.reshape(48, 24, 192), start_wd.reshape(24, 24, 768)
    )
    done_sq = done_sq.reshape(start_sq.shape).astype(jnp.float32)
    done_wd = done_wd.reshape(start_wd.shape).astype(jnp.float32)
    update_sq = (0.2 * math.sqrt(768) * done_sq).astype(jnp.bfloat16)
    update_wd = (0.2 * math.sqrt(3072) * done_wd).astype(jnp.bfloat16)
    keep = 1.0 - learning_rate * weight_decay
    weight_sq = weights_square * keep - learning_rate * update_sq.astype(jnp.float32)
    weight_wd = weights_wide * keep - learning_rate * update_wd.astype(jnp.float32)
    return (moment_sq, moment_wd, update_sq, update_wd, weight_sq, weight_wd)


def solution(mesh):
    spec = P(None, None, ("shard", "section"), "tensor")
    return jax.shard_map(
        local, mesh=mesh, in_specs=(spec,) * 6, out_specs=(spec,) * 6, check_vma=False
    )
```
